256 devices in a mesh: dp: 32 (over x_lo, z, core), tensor: 8 (over y, x_hi).
Axes of the slice: x: 4 (x_hi: 2, x_lo: 2; x = x_hi * 2 + x_lo), y: 4, z: 8, core: 2. Of those that a mesh axis runs over, the one named last changes fastest.
Arguments:
- tokens: bfloat16 [6144, 2048], P(('dp', 'tensor')), may hold values from -6 to 6
- grad_hidden: bfloat16 [6144, 5504], P('dp', 'tensor'), may hold values from -0.078125 to 0.078125
- width_in: bfloat16 [2048, 1024], P(None, 'tensor'), may hold values from -0.125 to 0.125
- gate_small: bfloat16 [1024, 2752], P(None, 'tensor'), may hold values from -0.1875 to 0.1875
- up_small: bfloat16 [1024, 2752], P(None, 'tensor'), may hold values from -0.1875 to 0.1875
- width_hidden: bfloat16 [5504, 2752], P('tensor'), may hold values from -0.109375 to 0.109375
Outputs:
- grad_width_in: float32 [2048, 1024], P('dp', 'tensor')
- grad_gate_small: float32 [1024, 2752], P('dp', 'tensor')
- grad_up_small: float32 [1024, 2752], P('dp', 'tensor')
- grad_width_hidden: float32 [5504, 2752], P('tensor', 'dp')
The draws below stay inside these ranges and needn't reach their ends.
All inputs are finite; a program needn't handle non-finite values.
Results may differ from the reference program's by a relative error of at most 0.0085.
Values may be sent and summed in bfloat16 or wider, within the bound.
No kernel may reach another device: no remote copies, remote signals or barrier semaphores. Data moves between devices by JAX's collectives and lax.ppermute only.
A program may use at most 64 MiB of HBM per device.

```python
import jax
import jax.numpy as jnp

D = 2048
DS = 1024
FS = 2752
FF = 5504
TOKENS = 6144


def shard_levels(rng, dims, shards, least, high):
    loudness = 1.0
    for position, parts in shards:
        steps = jax.random.uniform(jax.random.fold_in(jax.random.fold_in(rng, 6), position), (parts,), jnp.float32, least / len(shards), high / len(shards))
        loudness = loudness * jnp.repeat(jnp.exp(steps), dims[position] // parts).reshape((-1,) + (1,) * (len(dims) - 1 - position))
    return loudness


def noise(key, shape, deviation, bound, split=(), held_as=jnp.bfloat16):
    entries = deviation * jax.random.normal(key, shape, jnp.float32)
    if split:
        entries = entries * shard_levels(key, shape, split, -0.22, 0.18)
    return jnp.clip(entries, -bound, bound).astype(held_as)


def setup_inputs(seed: int = 0) -> dict:
    arg_keys = jax.random.split(jax.random.key(seed), 7)
    return {
        "tokens": noise(arg_keys[0], (TOKENS, D), 1.0, 6.0, ((0, 256),)),
        "grad_hidden": noise(arg_keys[1], (TOKENS, FF), (TOKENS ** -0.5), 0.078125, ((0, 32), (1, 8))),
        "width_in": noise(arg_keys[2], (D, DS), D ** -0.5, 0.125, ((1, 8),)),
        "gate_small": noise(arg_keys[3], (DS, FS), DS ** -0.5, 0.1875, ((1, 8),)),
        "up_small": noise(arg_keys[4], (DS, FS), DS ** -0.5, 0.1875, ((1, 8),)),
        "width_hidden": noise(arg_keys[5], (FF, FS), FS ** -0.5, 0.109375, ((0, 8),)),
    }


def reference(tokens, grad_hidden, width_in, gate_small, up_small, width_hidden):
    narrow = jnp.dot(tokens, width_in, preferred_element_type=jnp.float32).astype(jnp.bfloat16)
    gate_low = jnp.dot(narrow, gate_small, preferred_element_type=jnp.float32).astype(jnp.bfloat16)
    up_low = jnp.dot(narrow, up_small, preferred_element_type=jnp.float32).astype(jnp.bfloat16)
    gate_big = jnp.dot(gate_low, width_hidden.T, preferred_element_type=jnp.float32)
    up_big = jnp.dot(up_low, width_hidden.T, preferred_element_type=jnp.float32)
    upstream = grad_hidden.astype(jnp.float32)
    sig = jax.nn.sigmoid(gate_big)
    d_gate = (upstream * up_big * sig * (1.0 + gate_big * (1.0 - sig))).astype(jnp.bfloat16)
    d_up = (upstream * gate_big * sig).astype(jnp.bfloat16)
    grad_width_hidden = jnp.dot(d_gate.T, gate_low, preferred_element_type=jnp.float32) + jnp.dot(d_up.T, up_low, preferred_element_type=jnp.float32)
    d_gate_low = jnp.dot(d_gate, width_hidden, preferred_element_type=jnp.float32).astype(jnp.bfloat16)
    d_up_low = jnp.dot(d_up, width_hidden, preferred_element_type=jnp.float32).astype(jnp.bfloat16)
    grad_gate_small = jnp.dot(narrow.T, d_gate_low, preferred_element_type=jnp.float32)
    grad_up_small = jnp.dot(narrow.T, d_up_low, preferred_element_type=jnp.float32)
    d_narrow = (jnp.dot(d_gate_low, gate_small.T, preferred_element_type=jnp.float32) + jnp.dot(d_up_low, up_small.T, preferred_element_type=jnp.float32)).astype(jnp.bfloat16)
    grad_width_in = jnp.dot(tokens.T, d_narrow, preferred_element_type=jnp.float32)
    return (grad_width_in, grad_gate_small, grad_up_small, grad_width_hidden)
```

```python
import jax
import jax.numpy as jnp
from jax import lax
from jax.sharding import Mesh
from jax.sharding import PartitionSpec as P

F32 = jnp.float32
BF16 = jnp.bfloat16
X = ("xl", "xh")


def dot(left, right, dims):
    return lax.dot_general(left, right, (dims, ((), ())), preferred_element_type=F32)


def seat(axis, i):
    return (i % 2) * 2 + i // 2 if axis == X else i


def shift(value, axis, size, step):
    perm = [(seat(axis, i), seat(axis, (i + step) % size)) for i in range(size)]
    return lax.ppermute(value, axis, perm)


def swap(value, axis):
    return shift(value, axis, 2, 1)


def pick(index, first, second):
    return jnp.where(index == 0, first, second)


def ordered(index, own, other, axis):
    return pick(
        index, jnp.concatenate([own, other], axis), jnp.concatenate([other, own], axis)
    )


def place(canvas, piece, *start):
    return lax.dynamic_update_slice(canvas, piece, start)


def gather_four(value, axis, index, canvas, put):
    canvas = put(canvas, value, index)
    for step in (1, 3, 2):
        canvas = put(canvas, shift(value, axis, 4, step), (index - step) % 4)
    return canvas


def scatter_four(piece_of, axis, index):
    total = piece_of(index).astype(F32)
    for step in (1, 3, 2):
        total = total + shift(piece_of((index + step) % 4).astype(BF16), axis, 4, step).astype(F32)
    return total


def gather_ring(value, z, canvas, put):
    up = down = value
    canvas = put(canvas, value, z)
    for k in range(1, 5):
        up = shift(up, "z", 8, 1)
        if k < 4:
            down = shift(down, "z", 8, -1)
        canvas = put(canvas, up, (z - k) % 8)
        if k < 4:
            canvas = put(canvas, down, (z + k) % 8)
    return canvas


def scatter_ring(piece_of, z):
    up = piece_of((z + 4) % 8).astype(BF16)
    down = piece_of((z - 3) % 8).astype(BF16)
    for k in (3, 2, 1):
        up = (shift(up, "z", 8, 1).astype(F32) + piece_of((z + k) % 8)).astype(BF16)
        down = shift(down, "z", 8, -1)
        if k > 1:
            down = (down.astype(F32) + piece_of((z - k + 1) % 8)).astype(BF16)
    up = shift(up, "z", 8, 1)
    return piece_of(z) + up.astype(F32) + down.astype(F32)


def on_device(tokens, grad_hidden, width_in, gate_small, up_small, width_hidden):
    xl, z, c, y, xh = (lax.axis_index(a) for a in ("xl", "z", "c", "y", "xh"))
    x = xh * 2 + xl
    own, d_in = tokens.shape
    rows = own * 8
    wide = width_in.shape[1]
    ds = wide * 8
    fs = gate_small.shape[1]
    ff = width_hidden.shape[0]
    half, quarter = ff // 2, ff // 4
    part = ds // 32
    slot = fs // 4

    pair = ordered(xh, tokens, swap(tokens, "xh"), 0)
    all_tokens = gather_four(
        pair,
        "y",
        y,
        jnp.zeros((rows, d_in), BF16),
        lambda canvas, piece, i: place(canvas, piece, i * (2 * own), 0),
    )

    tz = (z % 4) * 2 + z // 4
    row0 = tz * wide + (xl * 2 + c) * part
    mine = jnp.concatenate(
        [lax.dynamic_slice_in_dim(m, row0, part, 0) for m in (gate_small, up_small)], 0
    )
    mine2 = ordered(xh, mine[None], swap(mine, "xh")[None], 0)
    proj = gather_four(
        mine2,
        "y",
        y,
        jnp.zeros((8, 2 * part, fs), BF16),
        lambda canvas, piece, i: place(canvas, piece, i * 2, 0, 0),
    )
    proj = jnp.transpose(proj, (1, 0, 2)).reshape(2 * part, 8 * fs)
    wt = dot(width_hidden, proj, ((1,), (1,))).astype(BF16)
    wt = wt.reshape(2, half, 2 * part)
    keep, send = pick(c, wt[0], wt[1]), pick(c, wt[1], wt[0])
    wt = ordered(c, keep[None], swap(send, "c")[None], 0)
    lo, hi = wt[:, :quarter], wt[:, quarter:]
    keep, send = pick(xl, lo, hi), pick(xl, hi, lo)
    wt = ordered(xl, keep[None], swap(send, "xl")[None], 0)
    blocks = [
        jnp.concatenate([wt[i, j, :, g * part : (g + 1) * part] for i in (0, 1) for j in (0, 1)], 1)
        for g in (0, 1)
    ]
    wt = jnp.concatenate(blocks, 0)
    wt = gather_ring(
        wt,
        z,
        jnp.zeros((2 * quarter, ds), BF16),
        lambda canvas, piece, i: place(canvas, piece, 0, i * wide),
    )

    lo, hi = grad_hidden[:, :half], grad_hidden[:, half:]
    keep, send = pick(c, lo, hi), pick(c, hi, lo)
    gh = jnp.stack([keep, swap(send, "c")])
    lo, hi = gh[:, :, :quarter], gh[:, :, quarter:]
    keep, send = pick(xl, lo, hi), pick(xl, hi, lo)
    gh = ordered(xl, keep[:, None], swap(send, "xl")[:, None], 1).reshape(4 * rows, quarter)

    narrow = dot(all_tokens, width_in, ((1,), (0,))).astype(BF16)
    narrow = gather_four(
        narrow,
        X,
        x,
        jnp.zeros((2 * rows, 2, wide), BF16).reshape(2 * rows, 2 * wide),
        lambda canvas, piece, i: place(canvas, piece, (i % 2) * rows, (i // 2) * wide),
    )

    def put_narrow(canvas, piece, i):
        canvas = place(canvas, piece[:, :wide], 0, i * wide)
        return place(canvas, piece[:, wide:], 0, (4 + i) * wide)

    narrow = gather_four(narrow, "y", y, jnp.zeros((2 * rows, ds), BF16), put_narrow)
    narrow = jnp.concatenate([narrow, swap(narrow, "c")], 0)

    gate_big = dot(narrow, wt[:quarter], ((1,), (1,)))
    up_big = dot(narrow, wt[quarter:], ((1,), (1,)))
    upstream = gh.astype(F32)
    sig = jax.nn.sigmoid(gate_big)
    d_gate = (upstream * up_big * sig * (1.0 + gate_big * (1.0 - sig))).astype(BF16)
    d_up = (upstream * gate_big * sig).astype(BF16)
    d_both = jnp.concatenate([d_gate, d_up], 1)

    m_part = dot(narrow, d_both, ((0,), (0,)))
    m_part = m_part.reshape(2, 2, 2, 2, wide // 2, 2 * quarter)

    def m_piece(i):
        piece = lax.dynamic_slice(
            m_part,
            ((i // 2) % 2, 0, i // 4, i % 2, 0, 0),
            (1, 2, 1, 1, wide // 2, 2 * quarter),
        )
        return piece.reshape(2, wide // 2, 2 * quarter)

    m_own = scatter_ring(m_piece, z).astype(BF16)

    back = dot(d_both, wt, ((1,), (0,))).reshape(2, 2 * rows, ds)
    back = back[0] + swap(back[1].astype(BF16), "c").astype(F32)
    back = scatter_four(
        lambda i: lax.dynamic_slice(back, ((i % 2) * rows, (i // 2) * 4 * wide), (rows, 4 * wide)),
        X,
        x,
    )
    d_narrow = scatter_four(
        lambda i: lax.dynamic_slice(back, (0, i * wide), (rows, wide)), "y", y
    ).astype(BF16)
    term = dot(all_tokens, d_narrow, ((0,), (0,))).reshape(2, 8, 2, d_in // 32, wide)
    keep, send = pick(c, term[:, :, 0], term[:, :, 1]), pick(c, term[:, :, 1], term[:, :, 0])
    term = keep + swap(send.astype(BF16), "c").astype(F32)
    keep, send = pick(xl, term[0], term[1]), pick(xl, term[1], term[0])
    term = keep + swap(send.astype(BF16), "xl").astype(F32)
    grad_width_in = scatter_ring(
        lambda i: lax.dynamic_slice_in_dim(term, i, 1, 0).reshape(d_in // 32, wide), z
    )

    wh = width_hidden.reshape(2, 2, quarter, 8 * fs)
    wh = pick(c, pick(xl, wh[0, 0], wh[0, 1]), pick(xl, wh[1, 0], wh[1, 1]))
    wh = jnp.transpose(wh.reshape(quarter, 4, 2, fs), (2, 1, 0, 3))
    wh = wh.reshape(8, quarter, fs)
    m_rows = m_own.reshape(2, 2, part, 2 * quarter)

    def small_term(cols):
        rows_of = jnp.broadcast_to(cols.reshape(1, 4 * part, quarter), (8, 4 * part, quarter))
        out = lax.dot_general(
            rows_of, wh, (((2,), (1,)), ((0,), (0,))), preferred_element_type=F32
        )
        return out.reshape(2, 4, 2, 2, part, fs)

    small = jnp.stack([small_term(m_rows[..., :quarter]), small_term(m_rows[..., quarter:])], 2)
    keep, send = (
        pick(c, small[..., 0, :, :], small[..., 1, :, :]),
        pick(c, small[..., 1, :, :], small[..., 0, :, :]),
    )
    small = keep + swap(send.astype(BF16), "c").astype(F32)
    small = scatter_four(
        lambda i: lax.dynamic_slice(
            small, (i // 2, 0, 0, i % 2, 0, 0), (1, 4, 2, 1, part, fs)
        ).reshape(4, 2, part, fs),
        X,
        x,
    )
    small = scatter_four(
        lambda i: lax.dynamic_slice_in_dim(small, i, 1, 0).reshape(2, part, fs), "y", y
    )
    grad_gate_small, grad_up_small = small[0], small[1]

    def fetch():
        block = lax.dynamic_slice_in_dim(pick(c, gate_small, up_small), z * wide, wide, 0)
        block = pick(xl, block[:, : fs // 2], block[:, fs // 2 :])
        return jnp.transpose(block.reshape(wide, 2, slot), (1, 2, 0))

    order = ("xl", "z", "c", "y", "xh")
    perm = []
    for i in range(256):
        sxl, sz, sc, sy, sxh = i // 128, i // 16 % 8, i // 8 % 2, i // 2 % 4, i % 2
        dz = (sy % 2) * 4 + sxh * 2 + sxl
        perm.append((i, (((sy // 2) * 8 + dz) * 2 + sc) * 8 + sz))
    cols = lax.ppermute(fetch(), order, perm)

    cols = gather_four(
        cols[None],
        X,
        x,
        jnp.zeros((2, 2, slot, 2 * wide), BF16),
        lambda canvas, piece, i: place(canvas, piece, i % 2, 0, 0, (i // 2) * wide),
    )
    cols = gather_four(
        cols,
        "y",
        y,
        jnp.zeros((2, 2, slot, ds), BF16),
        lambda canvas, piece, i: place(canvas, piece, 0, 0, 0, i * 2 * wide),
    )
    other = swap(cols, "c")
    cols_g, cols_u = pick(c, cols, other), pick(c, other, cols)

    m_all = gather_ring(
        m_own[:, None],
        z,
        jnp.zeros((2, 8, wide // 2, 2 * quarter), BF16),
        lambda canvas, piece, i: place(canvas, piece, 0, i, 0, 0),
    ).reshape(ds, 2 * quarter)

    def hidden_for(i, j):
        return dot(m_all[:, :quarter], cols_g[i, j], ((0,), (1,))) + dot(
            m_all[:, quarter:], cols_u[i, j], ((0,), (1,))
        )

    hid = [[hidden_for(i, j) for j in (0, 1)] for i in (0, 1)]
    to0, to1 = jnp.stack([hid[0][0], hid[1][0]]), jnp.stack([hid[0][1], hid[1][1]])
    keep, send = pick(c, to0, to1), pick(c, to1, to0).astype(BF16)
    hid = ordered(c, keep[:, None], swap(send, "c")[:, None].astype(F32), 1)
    keep, send = pick(xl, hid[0], hid[1]), pick(xl, hid[1], hid[0]).astype(BF16)
    hid = ordered(xl, keep[:, None], swap(send, "xl")[:, None].astype(F32), 1)
    hidden = hid.reshape(ff, slot)
    return (grad_width_in, grad_gate_small, grad_up_small, hidden)


def solution(mesh):
    grid = Mesh(mesh.devices.reshape(2, 8, 2, 4, 2), ("xl", "z", "c", "y", "xh"))
    dp, tensor = ("xl", "z", "c"), ("y", "xh")
    return jax.shard_map(
        on_device,
        mesh=grid,
        in_specs=(
            P(dp + tensor, None),
            P(dp, tensor),
            P(None, tensor),
            P(None, tensor),
            P(None, tensor),
            P(tensor, None),
        ),
        out_specs=(P(dp, tensor), P(dp, tensor), P(dp, tensor), P(tensor, dp)),
        check_vma=False,
    )
```

```python
import jax
import jax.numpy as jnp
from jax import lax
from jax.sharding import Mesh
from jax.sharding import PartitionSpec as P

F32 = jnp.float32
BF16 = jnp.bfloat16
CHIPS = ("xl", "y", "xh")


def dot(left, right, dims):
    return lax.dot_general(left, right, (dims, ((), ())), preferred_element_type=F32)


def shift(value, axis, size, step):
    return lax.ppermute(value, axis, [(i, (i + step) % size) for i in range(size)])


def batched(left, right, left_dim, right_dim):
    dims = (((left_dim,), (right_dim,)), ((0,), (0,)))
    return lax.dot_general(left, right, dims, preferred_element_type=F32)


def swap(value, axis):
    return shift(value, axis, 2, 1)


def pick(index, first, second):
    return jnp.where(index == 0, first, second)


def ordered(index, own, other, axis):
    return pick(
        index, jnp.concatenate([own, other], axis), jnp.concatenate([other, own], axis)
    )


def place(canvas, piece, *start):
    return lax.dynamic_update_slice(canvas, piece, start)


def gather_four(value, axis, index, canvas, put):
    canvas = put(canvas, value, index)
    for step in (1, 3, 2):
        canvas = put(canvas, shift(value, axis, 4, step), (index - step) % 4)
    return canvas


def exchange(pieces, axes):
    return lax.all_to_all(pieces, axes, 0, 0, tiled=True)


def gather(value, axes, size):
    return exchange(jnp.broadcast_to(value[None], (size,) + value.shape), axes)


def on_device(tokens, grad_hidden, width_in, gate_small, up_small, width_hidden):
    xl, z, c, y, xh = (lax.axis_index(a) for a in ("xl", "z", "c", "y", "xh"))
    own, d_in = tokens.shape
    rows = own * 8
    wide = width_in.shape[1]
    ds = wide * 8
    fs = gate_small.shape[1]
    ff = width_hidden.shape[0]
    quarter = ff // 4
    part = ds // 32
    slot = fs // 4

    pair = ordered(xh, tokens, swap(tokens, "xh"), 0)
    all_tokens = gather_four(
        pair,
        "y",
        y,
        jnp.zeros((rows, d_in), BF16),
        lambda canvas, piece, i: place(canvas, piece, i * (2 * own), 0),
    )

    row0 = z * wide + (xl * 2 + c) * part
    mine = jnp.concatenate(
        [lax.dynamic_slice_in_dim(m, row0, part, 0) for m in (gate_small, up_small)], 0
    )
    mine2 = ordered(xh, mine[None], swap(mine, "xh")[None], 0)
    proj = gather_four(
        mine2,
        "y",
        y,
        jnp.zeros((8, 2 * part, fs), BF16),
        lambda canvas, piece, i: place(canvas, piece, i * 2, 0, 0),
    )
    proj = jnp.transpose(proj, (1, 0, 2)).reshape(2 * part, 8 * fs)
    wt = dot(width_hidden, proj, ((1,), (1,))).astype(BF16)
    wt = wt.reshape(2, 2, quarter, 2 * part)
    keep, send = pick(c, wt[:, 0], wt[:, 1]), pick(c, wt[:, 1], wt[:, 0])
    wt = ordered(c, keep[None], swap(send, "c")[None], 0)
    keep, send = pick(xl, wt[:, 0], wt[:, 1]), pick(xl, wt[:, 1], wt[:, 0])
    wt = ordered(xl, keep[None], swap(send, "xl")[None], 0)
    blocks = [
        jnp.concatenate([wt[i, j, :, g * part : (g + 1) * part] for i in (0, 1) for j in (0, 1)], 1)
        for g in (0, 1)
    ]
    wt = jnp.concatenate(blocks, 0)
    wt_blocks = gather(wt, "z", 8)
    wt = jnp.transpose(wt_blocks, (1, 0, 2)).reshape(2 * quarter, ds)

    gh = jnp.stack([grad_hidden[:, i * quarter : (i + 1) * quarter] for i in range(4)])
    gh = exchange(gh, ("xl", "c")).reshape(2, 2, rows, quarter)
    gh = jnp.stack([pick(c, gh[:, 0], gh[:, 1]), pick(c, gh[:, 1], gh[:, 0])])
    gh = gh.reshape(2, 2 * rows, quarter)

    narrow = dot(all_tokens, width_in, ((1,), (0,))).astype(BF16)
    narrow = gather(narrow, CHIPS, 16).reshape(2, 8, rows, wide)
    narrow = jnp.transpose(narrow, (0, 2, 1, 3)).reshape(2 * rows, ds)
    narrow = jnp.concatenate([narrow, swap(narrow, "c")], 0)

    gate_big = dot(narrow, wt[:quarter], ((1,), (1,)))
    up_big = dot(narrow, wt[quarter:], ((1,), (1,)))
    upstream = gh.reshape(4 * rows, quarter).astype(F32)
    sig = jax.nn.sigmoid(gate_big)
    d_gate = (upstream * up_big * sig * (1.0 + gate_big * (1.0 - sig))).astype(BF16)
    d_up = (upstream * gate_big * sig).astype(BF16)
    d_both = jnp.concatenate([d_gate, d_up], 1)

    m_part = dot(narrow, d_both, ((0,), (0,))).reshape(2, 8, 2 * part, 2 * quarter)
    m_part = exchange(jnp.transpose(m_part, (1, 0, 2, 3)).astype(BF16), "z")
    m_own = jnp.sum(m_part.astype(F32), 0).astype(BF16)
    m_all = gather(m_own, "z", 8)
    m_all = jnp.transpose(m_all, (1, 0, 2, 3)).reshape(ds, 2 * quarter)

    def back_of(d):
        rows_of = jnp.broadcast_to(d[None], (8,) + d.shape)
        return batched(rows_of, wt_blocks, 2, 1)

    other = back_of(d_both[2 * rows :]).astype(BF16)
    back = back_of(d_both[: 2 * rows]) + swap(other, "c").astype(F32)
    back = jnp.transpose(back.reshape(8, 2, rows, wide), (1, 0, 2, 3)).astype(BF16)
    back = exchange(back.reshape(16, rows, wide), CHIPS)
    d_narrow = jnp.sum(back.astype(F32), 0).astype(BF16)
    term = dot(all_tokens, d_narrow, ((0,), (0,))).astype(BF16)
    term = exchange(term.reshape(32, d_in // 32, wide), ("xl", "z", "c"))
    grad_width_in = jnp.sum(term.astype(F32), 0)

    wh = lax.dynamic_slice_in_dim(width_hidden, (xl * 2 + c) * quarter, quarter, 0)
    wh = jnp.stack([wh[:, i * fs : (i + 1) * fs] for i in range(8)])
    m_rows = m_own.reshape(2, 2, part, 2 * quarter)

    def small_of(m):
        m = jnp.stack([m[..., :quarter], m[..., quarter:]], 1).reshape(1, 4 * part, quarter)
        return batched(jnp.broadcast_to(m, (8, 4 * part, quarter)), wh, 2, 1)

    other = small_of(pick(c, m_rows[:, 1], m_rows[:, 0])).astype(BF16)
    small = small_of(pick(c, m_rows[:, 0], m_rows[:, 1])) + swap(other, "c").astype(F32)
    small = jnp.transpose(small.reshape(8, 2, 2 * part, fs), (1, 0, 2, 3)).astype(BF16)
    small = exchange(small.reshape(16, 2 * part, fs), CHIPS)
    small = jnp.sum(small.astype(F32), 0)
    grad_gate_small, grad_up_small = small[:part], small[part:]

    block = lax.dynamic_slice_in_dim(pick(c, gate_small, up_small), z * wide, wide, 0)
    block = pick(xl, block[:, : fs // 2], block[:, fs // 2 :])
    block = jnp.transpose(block.reshape(wide, 2, slot), (1, 2, 0))
    order = ("xl", "z", "c", "y", "xh")
    perm = []
    for i in range(256):
        sxl, sz, sc, sy, sxh = i // 128, i // 16 % 8, i // 8 % 2, i // 2 % 4, i % 2
        dz = (sy % 2) * 4 + sxh * 2 + sxl
        perm.append((i, (((sy // 2) * 8 + dz) * 2 + sc) * 8 + sz))
    cols = gather(lax.ppermute(block, order, perm), CHIPS, 16).reshape(2, 8, 2, slot, wide)
    cols = jnp.transpose(cols, (0, 2, 3, 1, 4)).reshape(4, slot, ds)
    other = swap(cols, "c")
    cols_g, cols_u = pick(c, cols, other), pick(c, other, cols)

    def hidden_of(m, cols):
        return batched(jnp.broadcast_to(m[None], (4,) + m.shape), cols, 1, 2)

    hidden = hidden_of(m_all[:, :quarter], cols_g) + hidden_of(m_all[:, quarter:], cols_u)
    hidden = exchange(hidden.astype(BF16), ("xl", "c")).astype(F32).reshape(ff, slot)
    return (grad_width_in, grad_gate_small, grad_up_small, hidden)


def solution(mesh):
    grid = Mesh(mesh.devices.reshape(2, 8, 2, 4, 2), ("xl", "z", "c", "y", "xh"))
    dp, tensor = ("xl", "z", "c"), ("y", "xh")
    return jax.shard_map(
        on_device,
        mesh=grid,
        in_specs=(
            P(dp + tensor, None),
            P(dp, tensor),
            P(None, tensor),
            P(None, tensor),
            P(None, tensor),
            P(tensor, None),
        ),
        out_specs=(P(dp, tensor), P(dp, tensor), P(dp, tensor), P(tensor, dp)),
        check_vma=False,
    )
```

```python
import jax
import jax.numpy as jnp
from jax import lax
from jax.sharding import Mesh
from jax.sharding import PartitionSpec as P

F32 = jnp.float32
BF16 = jnp.bfloat16
CHIPS = ("xl", "y", "xh")


def dot(left, right, dims):
    return lax.dot_general(left, right, (dims, ((), ())), preferred_element_type=F32)


def shift(value, axis, size, step):
    return lax.ppermute(value, axis, [(i, (i + step) % size) for i in range(size)])


def batched(left, right, left_dim, right_dim):
    dims = (((left_dim,), (right_dim,)), ((0,), (0,)))
    return lax.dot_general(left, right, dims, preferred_element_type=F32)


def swap(value, axis):
    return shift(value, axis, 2, 1)


def pick(index, first, second):
    return jnp.where(index == 0, first, second)


def ordered(index, own, other, axis):
    return pick(
        index, jnp.concatenate([own, other], axis), jnp.concatenate([other, own], axis)
    )


def place(canvas, piece, *start):
    return lax.dynamic_update_slice(canvas, piece, start)


def gather_four(value, axis, index, canvas, put):
    canvas = put(canvas, value, index)
    for step in (1, 3, 2):
        canvas = put(canvas, shift(value, axis, 4, step), (index - step) & 3)
    return canvas


def exchange(pieces, axes):
    return lax.all_to_all(pieces, axes, 0, 0, tiled=True)


def gather(value, axes, size):
    return exchange(jnp.broadcast_to(value[None], (size,) + value.shape), axes)


def gather_ring(value, z):
    up = down = value[None]
    canvas = jnp.zeros((8,) + value.shape, value.dtype)
    tail = (0,) * value.ndim
    canvas = place(canvas, up, z, *tail)
    for k in range(1, 5):
        up = shift(up, "z", 8, 1)
        if k < 4:
            down = shift(down, "z", 8, -1)
        canvas = place(canvas, up, (z - k) & 7, *tail)
        if k < 4:
            canvas = place(canvas, down, (z + k) & 7, *tail)
    return canvas


def scatter_ring(pieces, z):
    def piece(i):
        return lax.dynamic_index_in_dim(pieces, i & 7, 0, False)

    up, down = piece(z + 4).astype(BF16), piece(z - 3).astype(BF16)
    for k in (3, 2, 1):
        up = shift(up, "z", 8, 1)
        down = shift(down, "z", 8, -1)
        up = (up.astype(F32) + piece(z + k)).astype(BF16)
        if k > 1:
            down = (down.astype(F32) + piece(z - k + 1)).astype(BF16)
    up = shift(up, "z", 8, 1)
    return piece(z) + up.astype(F32) + down.astype(F32)


def after(value, *others):
    return lax.optimization_barrier((value,) + others)[0]


def step(tokens, grad_hidden, width_in, gate_small, up_small, width_hidden):
    xl, z, c, y, xh = (lax.axis_index(a) for a in ("xl", "z", "c", "y", "xh"))
    own, d_in = tokens.shape
    rows = own * 8
    wide = width_in.shape[1]
    ds = wide * 8
    fs = gate_small.shape[1]
    ff = width_hidden.shape[0]
    quarter = ff // 4
    part = ds // 32
    slot = fs // 4

    pair = ordered(xh, tokens, swap(tokens, "xh"), 0)
    all_tokens = gather_four(
        pair,
        "y",
        y,
        jnp.zeros((rows, d_in), BF16),
        lambda canvas, piece, i: place(canvas, piece, i * (2 * own), 0),
    )

    row0 = z * wide + (xl * 2 + c) * part
    mine = jnp.concatenate(
        [lax.dynamic_slice_in_dim(m, row0, part, 0) for m in (gate_small, up_small)], 0
    )
    proj = gather(mine, ("y", "xh"), 8)
    proj = jnp.transpose(proj, (1, 0, 2)).reshape(2 * part, 8 * fs)
    wt = dot(width_hidden, proj, ((1,), (1,))).astype(BF16)
    wt = wt.reshape(2, 2, quarter, 2 * part)
    keep, send = pick(c, wt[:, 0], wt[:, 1]), pick(c, wt[:, 1], wt[:, 0])
    wt = ordered(c, keep[None], swap(send, "c")[None], 0)
    keep, send = pick(xl, wt[:, 0], wt[:, 1]), pick(xl, wt[:, 1], wt[:, 0])
    wt = ordered(xl, keep[None], swap(send, "xl")[None], 0)
    blocks = [
        jnp.concatenate([wt[i, j, :, g * part : (g + 1) * part] for i in (0, 1) for j in (0, 1)], 1)
        for g in (0, 1)
    ]
    wt = jnp.concatenate(blocks, 0)
    wt_blocks = gather_ring(wt, z)
    wt = jnp.transpose(wt_blocks, (1, 0, 2)).reshape(2 * quarter, ds)

    narrow = dot(all_tokens, width_in, ((1,), (0,))).astype(BF16)

    gh = after(grad_hidden, narrow)
    gh = jnp.stack([gh[:, i * quarter : (i + 1) * quarter] for i in range(4)])
    gh = gh.reshape(2, 2, rows, quarter)
    keep, send = pick(c, gh[:, 0], gh[:, 1]), pick(c, gh[:, 1], gh[:, 0])
    gh = jnp.stack([keep, swap(send, "c")])
    keep, send = pick(xl, gh[:, 0], gh[:, 1]), pick(xl, gh[:, 1], gh[:, 0])
    gh = ordered(xl, keep[:, None], swap(send, "xl")[:, None], 1)

    narrow_part = narrow
    narrow = gather(narrow, CHIPS, 16).reshape(2, 8, rows, wide)
    narrow = jnp.transpose(narrow, (0, 2, 1, 3)).reshape(2 * rows, ds)
    narrow = jnp.concatenate([narrow, swap(narrow, "c")], 0)

    block = lax.dynamic_slice_in_dim(pick(c, after(gate_small, narrow_part), up_small), z * wide, wide, 0)
    block = pick(xl, block[:, : fs // 2], block[:, fs // 2 :])
    block = jnp.transpose(block.reshape(wide, 2, slot), (1, 2, 0))
    order = ("xl", "z", "c", "y", "xh")
    perm = []
    for i in range(256):
        sxl, sz, sc, sy, sxh = i // 128, i // 16 % 8, i // 8 % 2, i // 2 % 4, i % 2
        dz = (sy % 2) * 4 + sxh * 2 + sxl
        perm.append((i, (((sy // 2) * 8 + dz) * 2 + sc) * 8 + sz))
    cols = gather(lax.ppermute(block, order, perm), CHIPS, 16).reshape(2, 8, 2, slot, wide)
    cols = jnp.transpose(cols, (0, 2, 3, 1, 4)).reshape(4, slot, ds)
    other = swap(cols, "c")
    cols_g, cols_u = pick(c, cols, other), pick(c, other, cols)

    narrow = after(narrow, cols_g, cols_u)
    gate_big = dot(narrow, wt[:quarter], ((1,), (1,)))
    up_big = dot(narrow, wt[quarter:], ((1,), (1,)))
    upstream = gh.reshape(4 * rows, quarter).astype(F32)
    sig = jax.nn.sigmoid(gate_big)
    d_gate = (upstream * up_big * sig * (1.0 + gate_big * (1.0 - sig))).astype(BF16)
    d_up = (upstream * gate_big * sig).astype(BF16)
    d_both = jnp.concatenate([d_gate, d_up], 1)

    m_part = dot(narrow, d_both, ((0,), (0,))).reshape(2, 8, 2 * part, 2 * quarter)

    def back_of(d):
        rows_of = jnp.broadcast_to(d[None], (8,) + d.shape)
        return batched(rows_of, wt_blocks, 2, 1)

    other = back_of(d_both[2 * rows :]).astype(BF16)
    back = back_of(d_both[: 2 * rows]) + swap(other, "c").astype(F32)
    back = jnp.transpose(back.reshape(8, 2, rows, wide), (1, 0, 2, 3)).astype(BF16)
    back = back.reshape(16, rows, wide)
    m_own = scatter_ring(jnp.transpose(m_part, (1, 0, 2, 3)), z).astype(BF16)
    m_all = gather_ring(m_own, z)
    m_all = jnp.transpose(m_all, (1, 0, 2, 3)).reshape(ds, 2 * quarter)

    d_narrow = jnp.sum(exchange(back, CHIPS).astype(F32), 0).astype(BF16)
    term = dot(all_tokens, d_narrow, ((0,), (0,))).astype(BF16)
    term = exchange(term.reshape(32, d_in // 32, wide), ("xl", "z", "c"))
    grad_width_in = jnp.sum(term.astype(F32), 0)

    wh = lax.dynamic_slice_in_dim(width_hidden, (xl * 2 + c) * quarter, quarter, 0)
    m_rows = m_own.reshape(2, 2, part, 2 * quarter)

    def small_of(m):
        m = jnp.stack([m[..., :quarter], m[..., quarter:]], 1).reshape(4 * part, quarter)
        return jnp.transpose(dot(wh, m, ((0,), (1,))).reshape(8, fs, 4 * part), (0, 2, 1))

    other = small_of(pick(c, m_rows[:, 1], m_rows[:, 0])).astype(BF16)
    small = small_of(pick(c, m_rows[:, 0], m_rows[:, 1])) + swap(other, "c").astype(F32)
    small = jnp.transpose(small.reshape(8, 2, 2 * part, fs), (1, 0, 2, 3)).astype(BF16)
    small = exchange(small.reshape(16, 2 * part, fs), CHIPS)
    small = jnp.sum(small.astype(F32), 0)
    grad_gate_small, grad_up_small = small[:part], small[part:]

    def hidden_of(m, cols):
        return batched(jnp.broadcast_to(m[None], (4,) + m.shape), cols, 1, 2)

    hidden = hidden_of(m_all[:, :quarter], cols_g) + hidden_of(m_all[:, quarter:], cols_u)
    hidden = hidden.astype(BF16).reshape(2, 2, quarter, slot)
    keep, send = pick(c, hidden[:, 0], hidden[:, 1]), pick(c, hidden[:, 1], hidden[:, 0])
    hidden = ordered(c, keep[None], swap(send, "c")[None], 0)
    keep, send = pick(xl, hidden[:, 0], hidden[:, 1]), pick(xl, hidden[:, 1], hidden[:, 0])
    hidden = ordered(xl, keep[None], swap(send, "xl")[None], 0).astype(F32).reshape(ff, slot)
    return (grad_width_in, grad_gate_small, grad_up_small, hidden)


def solution(mesh):
    grid = Mesh(mesh.devices.reshape(2, 8, 2, 4, 2), ("xl", "z", "c", "y", "xh"))
    dp, tensor = ("xl", "z", "c"), ("y", "xh")
    return jax.shard_map(
        step,
        mesh=grid,
        in_specs=(
            P(dp + tensor, None),
            P(dp, tensor),
            P(None, tensor),
            P(None, tensor),
            P(None, tensor),
            P(tensor, None),
        ),
        out_specs=(P(dp, tensor), P(dp, tensor), P(dp, tensor), P(tensor, dp)),
        check_vma=False,
    )
```

```python
import jax
import jax.numpy as jnp
from jax import lax
from jax.sharding import Mesh
from jax.sharding import PartitionSpec as P

F32 = jnp.float32
BF16 = jnp.bfloat16
CHIPS = ("xl", "y", "xh")


def dot(left, right, dims):
    return lax.dot_general(left, right, (dims, ((), ())), preferred_element_type=F32)


def shift(value, axis, size, step):
    return lax.ppermute(value, axis, [(i, (i + step) % size) for i in range(size)])


def batched(left, right, left_dim, right_dim):
    dims = (((left_dim,), (right_dim,)), ((0,), (0,)))
    return lax.dot_general(left, right, dims, preferred_element_type=F32)


def swap(value, axis):
    return shift(value, axis, 2, 1)


def pick(index, first, second):
    return jnp.where(index == 0, first, second)


def ordered(index, own, other, axis):
    return pick(
        index, jnp.concatenate([own, other], axis), jnp.concatenate([other, own], axis)
    )


def place(canvas, piece, *start):
    return lax.dynamic_update_slice(canvas, piece, start)


def gather_four(value, axis, index, canvas, put):
    canvas = put(canvas, value, index)
    for step in (1, 3, 2):
        canvas = put(canvas, shift(value, axis, 4, step), (index - step) & 3)
    return canvas


def exchange(pieces, axes):
    return lax.all_to_all(pieces, axes, 0, 0, tiled=True)


def gather(value, axes, size):
    return exchange(jnp.broadcast_to(value[None], (size,) + value.shape), axes)


def gather_ring(value, z):
    tail = (0,) * value.ndim
    canvas = place(jnp.zeros((8,) + value.shape, value.dtype), value[None], z, *tail)

    def pass_on(k, carry):
        up, down, canvas = carry
        up, down = shift(up, "z", 8, 1), shift(down, "z", 8, -1)
        canvas = place(canvas, up, (z - 1 - k) & 7, *tail)
        return up, down, place(canvas, down, (z + 1 + k) & 7, *tail)

    return lax.fori_loop(0, 4, pass_on, (value[None], value[None], canvas))[2]


def after(value, *others):
    return lax.optimization_barrier((value,) + others)[0]


def step(tokens, grad_hidden, width_in, gate_small, up_small, width_hidden):
    xl, z, c, y, xh = (lax.axis_index(a) for a in ("xl", "z", "c", "y", "xh"))
    own, d_in = tokens.shape
    rows = own * 8
    wide = width_in.shape[1]
    ds = wide * 8
    fs = gate_small.shape[1]
    ff = width_hidden.shape[0]
    quarter = ff // 4
    part = ds // 32
    slot = fs // 4

    pair = ordered(xh, tokens, swap(tokens, "xh"), 0)
    all_tokens = gather_four(
        pair,
        "y",
        y,
        jnp.zeros((rows, d_in), BF16),
        lambda canvas, piece, i: place(canvas, piece, i * (2 * own), 0),
    )

    row0 = z * wide + (xl * 2 + c) * part
    mine = jnp.concatenate(
        [lax.dynamic_slice_in_dim(m, row0, part, 0) for m in (gate_small, up_small)], 0
    )
    proj = gather(mine, ("y", "xh"), 8)
    proj = jnp.transpose(proj, (1, 0, 2)).reshape(2 * part, 8 * fs)
    wt = dot(width_hidden, proj, ((1,), (1,))).astype(BF16)
    wt = wt.reshape(2, 2, quarter, 2 * part)
    keep, send = pick(c, wt[:, 0], wt[:, 1]), pick(c, wt[:, 1], wt[:, 0])
    wt = ordered(c, keep[None], swap(send, "c")[None], 0)
    keep, send = pick(xl, wt[:, 0], wt[:, 1]), pick(xl, wt[:, 1], wt[:, 0])
    wt = ordered(xl, keep[None], swap(send, "xl")[None], 0)
    blocks = [
        jnp.concatenate([wt[i, j, :, g * part : (g + 1) * part] for i in (0, 1) for j in (0, 1)], 1)
        for g in (0, 1)
    ]
    wt = jnp.concatenate(blocks, 0)
    wt_blocks = gather_ring(wt, z)
    wt = jnp.transpose(wt_blocks, (1, 0, 2)).reshape(2 * quarter, ds)

    narrow = dot(all_tokens, width_in, ((1,), (0,))).astype(BF16)

    gh = after(grad_hidden, narrow)
    gh = jnp.stack([gh[:, i * quarter : (i + 1) * quarter] for i in range(4)])
    gh = gh.reshape(2, 2, rows, quarter)
    keep, send = pick(c, gh[:, 0], gh[:, 1]), pick(c, gh[:, 1], gh[:, 0])
    gh = jnp.stack([keep, swap(send, "c")])
    keep, send = pick(xl, gh[:, 0], gh[:, 1]), pick(xl, gh[:, 1], gh[:, 0])
    gh = ordered(xl, keep[:, None], swap(send, "xl")[:, None], 1)

    narrow_part = narrow
    narrow = gather(narrow, CHIPS, 16).reshape(2, 8, rows, wide)
    narrow = jnp.transpose(narrow, (0, 2, 1, 3)).reshape(2 * rows, ds)
    narrow = jnp.concatenate([narrow, swap(narrow, "c")], 0)

    block = lax.dynamic_slice_in_dim(pick(c, after(gate_small, narrow_part), up_small), z * wide, wide, 0)
    block = pick(xl, block[:, : fs // 2], block[:, fs // 2 :])
    block = jnp.transpose(block.reshape(wide, 2, slot), (1, 2, 0))
    order = ("xl", "z", "c", "y", "xh")
    perm = []
    for i in range(256):
        sxl, sz, sc, sy, sxh = i // 128, i // 16 % 8, i // 8 % 2, i // 2 % 4, i % 2
        dz = (sy % 2) * 4 + sxh * 2 + sxl
        perm.append((i, (((sy // 2) * 8 + dz) * 2 + sc) * 8 + sz))
    cols = gather(lax.ppermute(block, order, perm), CHIPS, 16).reshape(2, 8, 2, slot, wide)
    cols = jnp.transpose(cols, (0, 2, 3, 1, 4)).reshape(4, slot, ds)
    other = swap(cols, "c")
    cols_g, cols_u = pick(c, cols, other), pick(c, other, cols)

    gate_big = dot(narrow, wt[:quarter], ((1,), (1,)))
    up_big = dot(narrow, wt[quarter:], ((1,), (1,)))
    upstream = gh.reshape(4 * rows, quarter).astype(F32)
    sig = jax.nn.sigmoid(gate_big)
    d_gate = (upstream * up_big * sig * (1.0 + gate_big * (1.0 - sig))).astype(BF16)
    d_up = (upstream * gate_big * sig).astype(BF16)
    d_both = jnp.concatenate([d_gate, d_up], 1)

    m_part = dot(narrow, d_both, ((0,), (0,))).reshape(2, 8, 2 * part, 2 * quarter)

    def back_of(d):
        rows_of = jnp.broadcast_to(d[None], (8,) + d.shape)
        return batched(rows_of, wt_blocks, 2, 1)

    other = back_of(d_both[2 * rows :]).astype(BF16)
    back = back_of(d_both[: 2 * rows]) + swap(other, "c").astype(F32)
    back = jnp.transpose(back.reshape(8, 2, rows, wide), (1, 0, 2, 3)).astype(BF16)
    back = back.reshape(16, rows, wide)
    m_part = exchange(jnp.transpose(m_part, (1, 0, 2, 3)).astype(BF16), "z")
    m_own = jnp.sum(m_part.astype(F32), 0).astype(BF16)
    m_all = gather_ring(m_own, z)
    m_all = jnp.transpose(m_all, (1, 0, 2, 3)).reshape(ds, 2 * quarter)

    d_narrow = jnp.sum(exchange(back, CHIPS).astype(F32), 0).astype(BF16)
    term = dot(all_tokens, d_narrow, ((0,), (0,))).astype(BF16)
    term = exchange(term.reshape(32, d_in // 32, wide), ("xl", "z", "c"))
    grad_width_in = jnp.sum(term.astype(F32), 0)

    wh = lax.dynamic_slice_in_dim(width_hidden, (xl * 2 + c) * quarter, quarter, 0)
    m_rows = m_own.reshape(2, 2, part, 2 * quarter)

    def small_of(m):
        m = jnp.stack([m[..., :quarter], m[..., quarter:]], 1).reshape(4 * part, quarter)
        return jnp.transpose(dot(wh, m, ((0,), (1,))).reshape(8, fs, 4 * part), (0, 2, 1))

    other = small_of(pick(c, m_rows[:, 1], m_rows[:, 0])).astype(BF16)
    small = small_of(pick(c, m_rows[:, 0], m_rows[:, 1])) + swap(other, "c").astype(F32)
    small = jnp.transpose(small.reshape(8, 2, 2 * part, fs), (1, 0, 2, 3)).astype(BF16)
    small = exchange(small.reshape(16, 2 * part, fs), CHIPS)
    small = jnp.sum(small.astype(F32), 0)
    grad_gate_small, grad_up_small = small[:part], small[part:]

    def hidden_of(m, cols):
        return batched(jnp.broadcast_to(m[None], (4,) + m.shape), cols, 1, 2)

    hidden = hidden_of(m_all[:, :quarter], cols_g) + hidden_of(m_all[:, quarter:], cols_u)
    hidden = hidden.astype(BF16).reshape(2, 2, quarter, slot)
    keep, send = pick(c, hidden[:, 0], hidden[:, 1]), pick(c, hidden[:, 1], hidden[:, 0])
    hidden = ordered(c, keep[None], swap(send, "c")[None], 0)
    keep, send = pick(xl, hidden[:, 0], hidden[:, 1]), pick(xl, hidden[:, 1], hidden[:, 0])
    hidden = ordered(xl, keep[None], swap(send, "xl")[None], 0).astype(F32).reshape(ff, slot)
    return (grad_width_in, grad_gate_small, grad_up_small, hidden)


def solution(mesh):
    grid = Mesh(mesh.devices.reshape(2, 8, 2, 4, 2), ("xl", "z", "c", "y", "xh"))
    dp, tensor = ("xl", "z", "c"), ("y", "xh")
    return jax.shard_map(
        step,
        mesh=grid,
        in_specs=(
            P(dp + tensor, None),
            P(dp, tensor),
            P(None, tensor),
            P(None, tensor),
            P(None, tensor),
            P(tensor, None),
        ),
        out_specs=(P(dp, tensor), P(dp, tensor), P(dp, tensor), P(tensor, dp)),
        check_vma=False,
    )
```

```python
import jax
import jax.numpy as jnp
from jax import lax
from jax.sharding import Mesh
from jax.sharding import PartitionSpec as P

F32 = jnp.float32
BF16 = jnp.bfloat16
CHIPS = ("xl", "y", "xh")


def dot(left, right, dims):
    return lax.dot_general(left, right, (dims, ((), ())), preferred_element_type=F32)


def shift(value, axis, size, step):
    return lax.ppermute(value, axis, [(i, (i + step) % size) for i in range(size)])


def batched(left, right, left_dim, right_dim):
    dims = (((left_dim,), (right_dim,)), ((0,), (0,)))
    return lax.dot_general(left, right, dims, preferred_element_type=F32)


def swap(value, axis):
    return shift(value, axis, 2, 1)


def pick(index, first, second):
    return jnp.where(index == 0, first, second)


def ordered(index, own, other, axis):
    return pick(
        index, jnp.concatenate([own, other], axis), jnp.concatenate([other, own], axis)
    )


def place(canvas, piece, *start):
    return lax.dynamic_update_slice(canvas, piece, start)


def gather_four(value, axis, index, canvas, put):
    canvas = put(canvas, value, index)
    for step in (1, 3, 2):
        canvas = put(canvas, shift(value, axis, 4, step), (index - step) & 3)
    return canvas


def exchange(pieces, axes):
    return lax.all_to_all(pieces, axes, 0, 0, tiled=True)


def gather(value, axes, size):
    return exchange(jnp.broadcast_to(value[None], (size,) + value.shape), axes)


def gather_line(value, z):
    tail = (0,) * value.ndim
    inner = [(i, i ^ 1) for i in range(8)]
    outer = [(i, (i + 1) & 7 if i & 1 else (i - 1) & 7) for i in range(8)]
    pair, side = z // 2, 2 * (z & 1) - 1
    other = lax.ppermute(value, "z", inner)
    last = ordered(z & 1, value[None], other[None], 0)
    canvas = jnp.zeros((4, 2) + value.shape, value.dtype)
    canvas = place(canvas, last[None], pair, 0, *tail)
    for perm, slot in ((outer, pair + side), (inner, pair - side), (outer, pair + 2)):
        last = lax.ppermute(last, "z", perm)
        canvas = place(canvas, last[None], slot & 3, 0, *tail)
    return canvas.reshape((8,) + value.shape)


def after(value, *others):
    return lax.optimization_barrier((value,) + others)[0]


def step(tokens, grad_hidden, width_in, gate_small, up_small, width_hidden):
    xl, z, c, y, xh = (lax.axis_index(a) for a in ("xl", "z", "c", "y", "xh"))
    own, d_in = tokens.shape
    rows = own * 8
    wide = width_in.shape[1]
    ds = wide * 8
    fs = gate_small.shape[1]
    ff = width_hidden.shape[0]
    quarter = ff // 4
    part = ds // 32
    slot = fs // 4

    row0 = z * wide + (xl * 2 + c) * part
    mine = jnp.concatenate(
        [lax.dynamic_slice_in_dim(m, row0, part, 0) for m in (gate_small, up_small)], 0
    )
    lanes = -(-fs // 128) * 128
    more = 2 * part * lanes // d_in
    mine = jnp.pad(mine, ((0, 0), (0, lanes - fs))).reshape(more, d_in)
    mine = jnp.concatenate([tokens, mine], 0)[None]
    both = gather_four(
        ordered(xh, mine, swap(mine, "xh"), 0),
        "y",
        y,
        jnp.zeros((8, own + more, d_in), BF16),
        lambda canvas, piece, i: place(canvas, piece, i * 2, 0, 0),
    )
    all_tokens = both[:, :own].reshape(rows, d_in)
    proj = both[:, own:].reshape(8, 2 * part, lanes)[:, :, :fs]
    proj = jnp.transpose(proj, (1, 0, 2)).reshape(2 * part, 8 * fs)
    wt = dot(width_hidden, proj, ((1,), (1,))).astype(BF16)
    wt = wt.reshape(2, 2, quarter, 2 * part)
    keep, send = pick(c, wt[:, 0], wt[:, 1]), pick(c, wt[:, 1], wt[:, 0])
    wt = ordered(c, keep[None], swap(send, "c")[None], 0)
    keep, send = pick(xl, wt[:, 0], wt[:, 1]), pick(xl, wt[:, 1], wt[:, 0])
    wt = ordered(xl, keep[None], swap(send, "xl")[None], 0)
    blocks = [
        jnp.concatenate([wt[i, j, :, g * part : (g + 1) * part] for i in (0, 1) for j in (0, 1)], 1)
        for g in (0, 1)
    ]
    wt = jnp.concatenate(blocks, 0)
    wt_blocks = gather(wt, "z", 8)
    wt = jnp.transpose(wt_blocks, (1, 0, 2)).reshape(2 * quarter, ds)

    narrow = dot(all_tokens, width_in, ((1,), (0,))).astype(BF16)

    gh = after(grad_hidden, narrow)
    gh = jnp.stack([gh[:, i * quarter : (i + 1) * quarter] for i in range(4)])
    gh = gh.reshape(2, 2, rows, quarter)
    keep, send = pick(c, gh[:, 0], gh[:, 1]), pick(c, gh[:, 1], gh[:, 0])
    gh = jnp.stack([keep, swap(send, "c")])
    keep, send = pick(xl, gh[:, 0], gh[:, 1]), pick(xl, gh[:, 1], gh[:, 0])
    gh = ordered(xl, keep[:, None], swap(send, "xl")[:, None], 1)

    narrow = gather(narrow, CHIPS, 16).reshape(2, 8, rows, wide)
    narrow = jnp.transpose(narrow, (0, 2, 1, 3)).reshape(2 * rows, ds)
    narrow = jnp.concatenate([narrow, swap(narrow, "c")], 0)

    block = lax.dynamic_slice_in_dim(pick(c, gate_small, up_small), z * wide, wide, 0)
    block = pick(xl, block[:, : fs // 2], block[:, fs // 2 :])
    block = jnp.transpose(block.reshape(wide, 2, slot), (1, 2, 0))
    order = ("xl", "z", "c", "y", "xh")
    perm = []
    for i in range(256):
        sxl, sz, sc, sy, sxh = i // 128, i // 16 % 8, i // 8 % 2, i // 2 % 4, i % 2
        dz = (sy % 2) * 4 + sxh * 2 + sxl
        perm.append((i, (((sy // 2) * 8 + dz) * 2 + sc) * 8 + sz))
    cols = gather(lax.ppermute(block, order, perm), CHIPS, 16).reshape(2, 8, 2, slot, wide)
    cols = jnp.transpose(cols, (0, 2, 3, 1, 4)).reshape(4, slot, ds)
    other = swap(cols, "c")
    cols_g, cols_u = pick(c, cols, other), pick(c, other, cols)

    gate_big = dot(narrow, wt[:quarter], ((1,), (1,)))
    up_big = dot(narrow, wt[quarter:], ((1,), (1,)))
    upstream = gh.reshape(4 * rows, quarter).astype(F32)
    sig = jax.nn.sigmoid(gate_big)
    d_gate = (upstream * up_big * sig * (1.0 + gate_big * (1.0 - sig))).astype(BF16)
    d_up = (upstream * gate_big * sig).astype(BF16)
    d_both = jnp.concatenate([d_gate, d_up], 1)

    m_part = dot(narrow, d_both, ((0,), (0,))).reshape(2, 8, 2 * part, 2 * quarter)

    def back_of(d):
        rows_of = jnp.broadcast_to(d[None], (8,) + d.shape)
        return batched(rows_of, wt_blocks, 2, 1)

    other = back_of(d_both[2 * rows :]).astype(BF16)
    back = back_of(d_both[: 2 * rows]) + swap(other, "c").astype(F32)
    back = jnp.transpose(back.reshape(8, 2, rows, wide), (1, 0, 2, 3)).astype(BF16)
    back = back.reshape(16, rows, wide)
    m_part = exchange(jnp.transpose(m_part, (1, 0, 2, 3)).astype(BF16), "z")
    m_own = jnp.sum(m_part.astype(F32), 0).astype(BF16)
    m_all = gather_line(m_own, z)
    m_all = jnp.transpose(m_all, (1, 0, 2, 3)).reshape(ds, 2 * quarter)

    d_narrow = jnp.sum(exchange(back, CHIPS).astype(F32), 0).astype(BF16)
    term = dot(all_tokens, d_narrow, ((0,), (0,))).astype(BF16)
    term = exchange(term.reshape(32, d_in // 32, wide), ("xl", "z", "c"))
    grad_width_in = jnp.sum(term.astype(F32), 0)

    wh = lax.dynamic_slice_in_dim(width_hidden, (xl * 2 + c) * quarter, quarter, 0)
    m_rows = m_own.reshape(2, 2, part, 2 * quarter)

    def small_of(m):
        m = jnp.stack([m[..., :quarter], m[..., quarter:]], 1).reshape(4 * part, quarter)
        return jnp.transpose(dot(wh, m, ((0,), (1,))).reshape(8, fs, 4 * part), (0, 2, 1))

    other = small_of(pick(c, m_rows[:, 1], m_rows[:, 0])).astype(BF16)
    small = small_of(pick(c, m_rows[:, 0], m_rows[:, 1])) + swap(other, "c").astype(F32)
    small = jnp.transpose(small.reshape(8, 2, 2 * part, fs), (1, 0, 2, 3)).astype(BF16)
    small = exchange(small.reshape(16, 2 * part, fs), CHIPS)
    small = jnp.sum(small.astype(F32), 0)
    grad_gate_small, grad_up_small = small[:part], small[part:]

    def hidden_of(m, cols):
        return batched(jnp.broadcast_to(m[None], (4,) + m.shape), cols, 1, 2)

    hidden = hidden_of(m_all[:, :quarter], cols_g) + hidden_of(m_all[:, quarter:], cols_u)
    hidden = hidden.astype(BF16).reshape(2, 2, quarter, slot)
    keep, send = pick(c, hidden[:, 0], hidden[:, 1]), pick(c, hidden[:, 1], hidden[:, 0])
    hidden = ordered(c, keep[None], swap(send, "c")[None], 0)
    keep, send = pick(xl, hidden[:, 0], hidden[:, 1]), pick(xl, hidden[:, 1], hidden[:, 0])
    hidden = ordered(xl, keep[None], swap(send, "xl")[None], 0).astype(F32).reshape(ff, slot)
    return (grad_width_in, grad_gate_small, grad_up_small, hidden)


def solution(mesh):
    grid = Mesh(mesh.devices.reshape(2, 8, 2, 4, 2), ("xl", "z", "c", "y", "xh"))
    dp, tensor = ("xl", "z", "c"), ("y", "xh")
    return jax.shard_map(
        step,
        mesh=grid,
        in_specs=(
            P(dp + tensor, None),
            P(dp, tensor),
            P(None, tensor),
            P(None, tensor),
            P(None, tensor),
            P(tensor, None),
        ),
        out_specs=(P(dp, tensor), P(dp, tensor), P(dp, tensor), P(tensor, dp)),
        check_vma=False,
    )
```

```python
import jax
import jax.numpy as jnp
from jax import lax
from jax.sharding import Mesh
from jax.sharding import PartitionSpec as P

F32 = jnp.float32
BF16 = jnp.bfloat16
CHIPS = ("xl", "y", "xh")


def dot(left, right, dims):
    return lax.dot_general(left, right, (dims, ((), ())), preferred_element_type=F32)


def shift(value, axis, size, step):
    return lax.ppermute(value, axis, [(i, (i + step) % size) for i in range(size)])


def batched(left, right, left_dim, right_dim):
    dims = (((left_dim,), (right_dim,)), ((0,), (0,)))
    return lax.dot_general(left, right, dims, preferred_element_type=F32)


def swap(value, axis):
    return shift(value, axis, 2, 1)


def pick(index, first, second):
    return jnp.where(index == 0, first, second)


def ordered(index, own, other, axis):
    return pick(
        index, jnp.concatenate([own, other], axis), jnp.concatenate([other, own], axis)
    )


def place(canvas, piece, *start):
    return lax.dynamic_update_slice(canvas, piece, start)


def gather_four(value, axis, index, canvas, put):
    canvas = put(canvas, value, index)
    for step in (1, 3, 2):
        canvas = put(canvas, shift(value, axis, 4, step), (index - step) & 3)
    return canvas


def exchange(pieces, axes):
    return lax.all_to_all(pieces, axes, 0, 0, tiled=True)


def gather(value, axes, size):
    return exchange(jnp.broadcast_to(value[None], (size,) + value.shape), axes)


def gather_line(value, z):
    tail = (0,) * value.ndim
    inner = [(i, i ^ 1) for i in range(8)]
    outer = [(i, (i + 1) & 7 if i & 1 else (i - 1) & 7) for i in range(8)]
    pair, side = z // 2, 2 * (z & 1) - 1
    other = lax.ppermute(value, "z", inner)
    last = ordered(z & 1, value[None], other[None], 0)
    canvas = jnp.zeros((4, 2) + value.shape, value.dtype)
    canvas = place(canvas, last[None], pair, 0, *tail)
    for perm, slot in ((outer, pair + side), (inner, pair - side), (outer, pair + 2)):
        last = lax.ppermute(last, "z", perm)
        canvas = place(canvas, last[None], slot & 3, 0, *tail)
    return canvas.reshape((8,) + value.shape)


def after(value, *others):
    return lax.optimization_barrier((value,) + others)[0]


def step(tokens, grad_hidden, width_in, gate_small, up_small, width_hidden):
    xl, z, c, y, xh = (lax.axis_index(a) for a in ("xl", "z", "c", "y", "xh"))
    own, d_in = tokens.shape
    rows = own * 8
    wide = width_in.shape[1]
    ds = wide * 8
    fs = gate_small.shape[1]
    ff = width_hidden.shape[0]
    quarter = ff // 4
    part = ds // 32
    slot = fs // 4

    row0 = z * wide + (xl * 2 + c) * part
    mine = jnp.concatenate(
        [lax.dynamic_slice_in_dim(m, row0, part, 0) for m in (gate_small, up_small)], 0
    )
    lanes = -(-fs // 128) * 128
    more = 2 * part * lanes // d_in
    mine = jnp.pad(mine, ((0, 0), (0, lanes - fs))).reshape(more, d_in)
    mine = jnp.concatenate([tokens, mine], 0)[None]
    both = gather_four(
        ordered(xh, mine, swap(mine, "xh"), 0),
        "y",
        y,
        jnp.zeros((8, own + more, d_in), BF16),
        lambda canvas, piece, i: place(canvas, piece, i * 2, 0, 0),
    )
    all_tokens = both[:, :own].reshape(rows, d_in)
    proj = both[:, own:].reshape(8, 2 * part, lanes)[:, :, :fs]
    proj = jnp.transpose(proj, (1, 0, 2)).reshape(2 * part, 8 * fs)
    wt = dot(width_hidden, proj, ((1,), (1,))).astype(BF16)
    wt = wt.reshape(2, 2, quarter, 2 * part)
    keep, send = pick(c, wt[:, 0], wt[:, 1]), pick(c, wt[:, 1], wt[:, 0])
    wt = ordered(c, keep[None], swap(send, "c")[None], 0)
    keep, send = pick(xl, wt[:, 0], wt[:, 1]), pick(xl, wt[:, 1], wt[:, 0])
    wt = ordered(xl, keep[None], swap(send, "xl")[None], 0)
    blocks = [
        jnp.concatenate([wt[i, j, :, g * part : (g + 1) * part] for i in (0, 1) for j in (0, 1)], 1)
        for g in (0, 1)
    ]
    wt = jnp.concatenate(blocks, 0)
    wt_blocks = gather(wt, "z", 8)
    wt = jnp.transpose(wt_blocks, (1, 0, 2)).reshape(2 * quarter, ds)

    narrow = dot(all_tokens, width_in, ((1,), (0,))).astype(BF16)

    gh = after(grad_hidden, narrow)
    gh = jnp.stack([gh[:, i * quarter : (i + 1) * quarter] for i in range(4)])
    gh = gh.reshape(2, 2, rows, quarter)
    keep, send = pick(c, gh[:, 0], gh[:, 1]), pick(c, gh[:, 1], gh[:, 0])
    gh = jnp.stack([keep, swap(send, "c")])
    keep, send = pick(xl, gh[:, 0], gh[:, 1]), pick(xl, gh[:, 1], gh[:, 0])
    gh = ordered(xl, keep[:, None], swap(send, "xl")[:, None], 1)

    narrow = gather(narrow, CHIPS, 16).reshape(2, 8, rows, wide)
    narrow = jnp.transpose(narrow, (0, 2, 1, 3)).reshape(2 * rows, ds)
    narrow = jnp.concatenate([narrow, swap(narrow, "c")], 0)

    block = lax.dynamic_slice_in_dim(pick(c, gate_small, up_small), z * wide, wide, 0)
    block = pick(xl, block[:, : fs // 2], block[:, fs // 2 :])
    block = jnp.transpose(block.reshape(wide, 2, slot), (1, 2, 0))
    order = ("xl", "z", "c", "y", "xh")
    perm = []
    for i in range(256):
        sxl, sz, sc, sy, sxh = i // 128, i // 16 % 8, i // 8 % 2, i // 2 % 4, i % 2
        dz = (sy % 2) * 4 + sxh * 2 + sxl
        perm.append((i, (((sy // 2) * 8 + dz) * 2 + sc) * 8 + sz))
    cols = lax.ppermute(block, order, perm)[None]
    cols = ordered(xl, cols, swap(cols, "xl"), 0)
    cols = ordered(xh, cols, swap(cols, "xh"), 3)
    cols = ordered(y & 1, cols, lax.ppermute(cols, "y", [(0, 1), (1, 0), (2, 3), (3, 2)]), 3)
    other = lax.ppermute(cols, "y", [(1, 2), (2, 1), (3, 0), (0, 3)])
    cols = ordered(y // 2, cols, other, 3)
    cols = cols.reshape(4, slot, ds)
    other = swap(cols, "c")
    cols_g, cols_u = pick(c, cols, other), pick(c, other, cols)

    gate_big = dot(narrow, wt[:quarter], ((1,), (1,)))
    up_big = dot(narrow, wt[quarter:], ((1,), (1,)))
    upstream = gh.reshape(4 * rows, quarter).astype(F32)
    sig = jax.nn.sigmoid(gate_big)
    d_gate = (upstream * up_big * sig * (1.0 + gate_big * (1.0 - sig))).astype(BF16)
    d_up = (upstream * gate_big * sig).astype(BF16)
    d_both = jnp.concatenate([d_gate, d_up], 1)

    m_part = dot(narrow, d_both, ((0,), (0,))).reshape(2, 8, 2 * part, 2 * quarter)

    def back_of(d):
        rows_of = jnp.broadcast_to(d[None], (8,) + d.shape)
        return batched(rows_of, wt_blocks, 2, 1)

    other = back_of(d_both[2 * rows :]).astype(BF16)
    back = back_of(d_both[: 2 * rows]) + swap(other, "c").astype(F32)
    back = jnp.transpose(back.reshape(8, 2, rows, wide), (1, 0, 2, 3)).astype(BF16)
    back = back.reshape(16, rows, wide)
    m_part = exchange(jnp.transpose(m_part, (1, 0, 2, 3)).astype(BF16), "z")
    m_own = jnp.sum(m_part.astype(F32), 0).astype(BF16)
    m_all = gather_line(m_own, z)
    m_all = jnp.transpose(m_all, (1, 0, 2, 3)).reshape(ds, 2 * quarter)

    d_narrow = jnp.sum(exchange(back, CHIPS).astype(F32), 0).astype(BF16)
    term = dot(all_tokens, d_narrow, ((0,), (0,))).astype(BF16)
    term = exchange(term.reshape(32, d_in // 32, wide), ("xl", "z", "c"))
    grad_width_in = jnp.sum(term.astype(F32), 0)

    wh = lax.dynamic_slice_in_dim(width_hidden, (xl * 2 + c) * quarter, quarter, 0)
    m_rows = m_own.reshape(2, 2, part, 2 * quarter)

    def small_of(m):
        m = jnp.stack([m[..., :quarter], m[..., quarter:]], 1).reshape(4 * part, quarter)
        return jnp.transpose(dot(wh, m, ((0,), (1,))).reshape(8, fs, 4 * part), (0, 2, 1))

    other = small_of(pick(c, m_rows[:, 1], m_rows[:, 0])).astype(BF16)
    small = small_of(pick(c, m_rows[:, 0], m_rows[:, 1])) + swap(other, "c").astype(F32)
    small = jnp.transpose(small.reshape(8, 2, 2 * part, fs), (1, 0, 2, 3)).astype(BF16)
    small = exchange(small.reshape(16, 2 * part, fs), CHIPS)
    small = jnp.sum(small.astype(F32), 0)
    grad_gate_small, grad_up_small = small[:part], small[part:]

    def hidden_of(m, cols):
        return batched(jnp.broadcast_to(m[None], (4,) + m.shape), cols, 1, 2)

    hidden = hidden_of(m_all[:, :quarter], cols_g) + hidden_of(m_all[:, quarter:], cols_u)
    hidden = hidden.astype(BF16).reshape(2, 2, quarter, slot)
    keep, send = pick(c, hidden[:, 0], hidden[:, 1]), pick(c, hidden[:, 1], hidden[:, 0])
    hidden = ordered(c, keep[None], swap(send, "c")[None], 0)
    keep, send = pick(xl, hidden[:, 0], hidden[:, 1]), pick(xl, hidden[:, 1], hidden[:, 0])
    hidden = ordered(xl, keep[None], swap(send, "xl")[None], 0).astype(F32).reshape(ff, slot)
    return (grad_width_in, grad_gate_small, grad_up_small, hidden)


def solution(mesh):
    grid = Mesh(mesh.devices.reshape(2, 8, 2, 4, 2), ("xl", "z", "c", "y", "xh"))
    dp, tensor = ("xl", "z", "c"), ("y", "xh")
    return jax.shard_map(
        step,
        mesh=grid,
        in_specs=(
            P(dp + tensor, None),
            P(dp, tensor),
            P(None, tensor),
            P(None, tensor),
            P(None, tensor),
            P(tensor, None),
        ),
        out_specs=(P(dp, tensor), P(dp, tensor), P(dp, tensor), P(tensor, dp)),
        check_vma=False,
    )
```
